512 devices in a mesh: dp: 16 (over z_lo, y), mp: 32 (over x, z_hi, core).
Axes of the slice: x: 4, y: 8, z: 8 (z_hi: 4, z_lo: 2; z = z_hi * 2 + z_lo), core: 2. Of those that a mesh axis runs over, the one named last changes fastest.
Arguments:
- out_grads: bfloat16 [2048, 28672], P('dp', 'mp'), may hold values from -6 to 6
- inputs: bfloat16 [2048, 8192], P('mp', 'dp'), may hold values from -6 to 6
- out_basis: bfloat16 [28672, 14336], P('mp', 'dp'), may hold values from -0.03125 to 0.03125
- in_basis: bfloat16 [8192, 8192], P('dp', 'mp'), may hold values from -0.0625 to 0.0625
- query_out: bfloat16 [128, 28672], P('dp', 'mp'), may hold values from -2.390625 to 2.390625
- query_in: bfloat16 [128, 8192], P('mp', 'dp'), may hold values from -2.390625 to 2.390625
- damping: float32 [1], replicated, may hold values from 0.5 to 2
Outputs:
- eigenvalues: float32 [14336, 8192], P('dp', 'mp')
- preconditioned: bfloat16 [4, 14336, 8192], P(None, 'dp', 'mp')
The draws below stay inside these ranges and needn't reach their ends.
All inputs are finite; a program needn't handle non-finite values.
Results may differ from the reference program's by a relative error of at most 0.033.
Values may be sent and summed in bfloat16 or wider, within the bound.
A program may use at most 64 MiB of HBM per device.

```python
import math
import jax
import jax.numpy as jnp
from jax import lax

DI = 8192
DO = 28672
KG = 14336
Q = 4
RANK = 32
TOKENS = 2048
SEQ = 1024
N_DP = 16
N_MP = 32


def shard_levels(own_key, extent, shards, smallest, top_value):
    factor_of, own = 1.0, jax.random.fold_in(own_key, 6)
    for axis_at, shards_of in shards:
        draws = jnp.exp(jax.random.uniform(jax.random.fold_in(own, axis_at), (shards_of,), jnp.float32, smallest / len(shards), top_value / len(shards)))
        factor_of = factor_of * jnp.repeat(draws, extent[axis_at] // shards_of).reshape([-1 if axis == axis_at else 1 for axis in range(len(extent))])
    return factor_of


def normal_values(key, dims, spread, bound, cuts=(), kind=jnp.bfloat16):
    drawn = jax.random.normal(key, dims, jnp.float32) * spread
    if len(cuts) > 0:
        drawn = shard_levels(key, dims, cuts, -0.22, 0.18) * drawn
    return jnp.clip(drawn, min=-bound, max=bound).astype(kind)


def setup_inputs(seed: int = 0) -> dict:
    seeds = jax.random.split(jax.random.key(seed), 8)
    return {
        "out_grads": normal_values(seeds[0], (TOKENS, DO), 1.0, 6.0, ((0, 16), (1, 32))),
        "inputs": normal_values(seeds[1], (TOKENS, DI), 1.0, 6.0, ((0, 32), (1, 16))),
        "out_basis": normal_values(seeds[2], (DO, KG), DO ** -0.5, 0.03125, ((0, 32), (1, 16))),
        "in_basis": normal_values(seeds[3], (DI, DI), DI ** -0.5, 0.0625, ((0, 16), (1, 32))),
        "query_out": normal_values(seeds[4], (Q * RANK, DO), 0.4, 2.390625, ((0, 16), (1, 32))),
        "query_in": normal_values(seeds[5], (Q * RANK, DI), 0.4, 2.390625, ((0, 32), (1, 16))),
        "damping": jnp.clip(jnp.exp(jax.random.uniform(seeds[6], (1,), jnp.float32, math.log(0.5), math.log(2.0))), 0.5, 2.0),
    }


def blocked_product(rows, basis, parts):
    width = rows.shape[1] // parts

    def step(total, index):
        piece = lax.dynamic_slice_in_dim(rows, index * width, width, 1)
        block = lax.dynamic_slice_in_dim(basis, index * width, width, 0)
        term = jnp.dot(piece, block, preferred_element_type=jnp.float32).astype(jnp.bfloat16)
        term = lax.optimization_barrier(term)
        return total + term.astype(jnp.float32), None

    start = jnp.zeros((rows.shape[0], basis.shape[1]), jnp.float32)
    total, _ = lax.scan(step, start, jnp.arange(parts, dtype=jnp.int32))
    return total.astype(jnp.bfloat16)


def reference(out_grads, inputs, out_basis, in_basis, query_out, query_in, damping):
    rot_grads = blocked_product(out_grads, out_basis, N_MP)
    rot_left = blocked_product(query_out, out_basis, N_MP)
    rot_inputs = blocked_product(inputs, in_basis, N_DP)
    rot_right = blocked_product(query_in, in_basis, N_DP)
    squares = jnp.zeros((KG, DI), jnp.float32)
    for seq_index in range(2):
        grad_seq = rot_grads[seq_index * SEQ:(seq_index + 1) * SEQ]
        input_seq = rot_inputs[seq_index * SEQ:(seq_index + 1) * SEQ]
        rotated = jnp.dot(grad_seq.T, input_seq, preferred_element_type=jnp.float32)
        squares = squares + rotated * rotated
    eigenvalues = squares / (2.0 * SEQ)
    shifted = eigenvalues + damping[0]

    def one_query(index):
        left = lax.dynamic_slice_in_dim(rot_left, index * RANK, RANK, 0)
        right = lax.dynamic_slice_in_dim(rot_right, index * RANK, RANK, 0)
        product = jnp.dot(left.T, right, preferred_element_type=jnp.float32)
        return (product / shifted).astype(jnp.bfloat16)

    preconditioned = lax.map(one_query, jnp.arange(Q, dtype=jnp.int32))
    return eigenvalues, preconditioned
```

```python
import jax
import jax.numpy as jnp
from jax import lax
from jax.experimental import pallas as pl
from jax.experimental.pallas import tpu as pltpu
from jax.sharding import PartitionSpec as P

BF = jnp.bfloat16
F32 = jnp.float32
MESH = pl.DeviceIdType.MESH
NT = (((1,), (1,)), ((), ()))

NY, NX, NH = 8, 4, 4
CHUNKS = ((0, 1), (1, 2), (3, 2), (5, 2), (7, 1))
QSLOT = 8
OFFSETS = (0, -1, 1, -2, 2, -3, 3, 4)
UP = {0: 1, 1: 3, 3: 5, 5: 7}
DOWN = {0: 2, 2: 4, 4: 6, 6: 7}
N_SEND, N_RECV = 180, 180


def kernel(
    g, q, b, xc, bi, damp, eig, pre,
    gk, qk, bt, bi2, pt, r1, s1, r2, rg,
    xk, px, rzx, sx, ryx, ox, rx, xf,
    ssem, rsem,
):
    dp, mp = lax.axis_index("dp"), lax.axis_index("mp")
    a, y = lax.div(dp, NY), lax.rem(dp, NY)
    x, h, c = lax.div(mp, 8), lax.rem(lax.div(mp, 2), NH), lax.rem(mp, 2)

    def dev(a=a, y=y, x=x, h=h, c=c):
        return {"dp": a * NY + y, "mp": (x * NH + h) * 2 + c}

    def wrap(v, n):
        return lax.rem(v + n, n)

    yd = [y] + [wrap(y + d, NY) for d in range(1, NY)]
    xd = [x] + [wrap(x + d, NX) for d in range(1, NX)]
    hd = [h] + [wrap(h + d, NH) for d in range(1, NH)]
    counts = [0, 0]
    sent = []

    def new_send():
        counts[0] += 1
        assert counts[0] <= N_SEND
        return ssem.at[counts[0] - 1]

    def new_recv(n=1):
        counts[1] += n
        assert counts[1] <= N_RECV
        return counts[1] - n

    def push(src, dst, to, recv, landing=None):
        copy = pltpu.make_async_remote_copy(
            src_ref=src, dst_ref=dst, send_sem=new_send(), recv_sem=recv,
            device_id=to, device_id_type=MESH,
        )
        copy.start()
        sent.append(copy)
        return arrival(dst if landing is None else landing, recv)

    def arrival(landing, recv):
        return pltpu.make_async_copy(landing, landing, recv)

    barrier = pltpu.get_barrier_semaphore()
    partners = [dev(c=1 - c), dev(a=1 - a), dev(a=1 - a, c=1 - c)]
    partners += [dev(x=xd[d]) for d in (1, 3, 2)]
    partners += [dev(h=hd[d]) for d in (1, 3, 2)]
    partners += [dev(y=yd[d], c=cc) for d in (1, 7, 2, 6, 3, 5, 4) for cc in (c, 1 - c)]
    for to in partners:
        pl.semaphore_signal(barrier, inc=1, device_id=to, device_id_type=MESH)
    pl.semaphore_wait(barrier, len(partners))

    g0 = new_recv(2)
    q0 = new_recv(2)
    own_send = [new_send() for _ in range(2)]
    own_q = qk.at[c, a * NY + y]

    def to_other_core():
        return (
            pltpu.make_async_remote_copy(
                src_ref=g, dst_ref=gk.at[0, c], send_sem=own_send[0],
                recv_sem=rsem.at[g0 + c], device_id=dev(c=1 - c), device_id_type=MESH,
            ),
            pltpu.make_async_remote_copy(
                src_ref=q, dst_ref=own_q, send_sem=own_send[1],
                recv_sem=rsem.at[q0 + c], device_id=dev(c=1 - c), device_id_type=MESH,
            ),
        )

    @pl.when(c == a)
    def _():
        pltpu.make_async_copy(g, gk.at[0, c], rsem.at[g0 + c]).start()
        pltpu.make_async_copy(q, own_q, rsem.at[q0 + c]).start()

    @pl.when(c != a)
    def _():
        for copy in to_other_core():
            copy.start()

    push(g, gk.at[0, c], dev(a=1 - a, c=a), rsem.at[g0 + c])
    push(q, own_q, dev(a=1 - a, c=a), rsem.at[q0 + c])

    here = xk.at[x * NH + h]
    local = pltpu.make_async_copy(xc, here, rsem.at[new_recv()])
    local.start()
    x_h = []
    for d in (1, 3, 2):
        x_h.append(
            push(xc, here, dev(h=hd[d]), rsem.at[new_recv()], xk.at[x * NH + hd[NH - d]])
        )
    bi_local = pltpu.make_async_copy(bi, bi2.at[c], rsem.at[new_recv()])
    bi_local.start()
    bi_other = push(bi, bi2.at[c], dev(c=1 - c), rsem.at[new_recv()], bi2.at[1 - c])

    eye = (
        lax.broadcasted_iota(jnp.int32, (128, 128), 0)
        == lax.broadcasted_iota(jnp.int32, (128, 128), 1)
    ).astype(F32).astype(BF)

    for j in range(7):
        block = lax.dot_general(
            eye, b[:, j * 128 : (j + 1) * 128], NT, preferred_element_type=F32
        )
        bt[c, j * 128 : (j + 1) * 128, :] = block.astype(BF)
    bt_other = push(bt.at[c], bt.at[c], dev(c=1 - c), rsem.at[new_recv()], bt.at[1 - c])
    qk[:, pl.ds((1 - c) * NY, NY)] = jnp.zeros((2, NY, 8, 896), BF)

    ring = {}
    ring_recv = {(s, cb): new_recv() for s in range(1, 8) for cb in range(2)}

    def forward(slot, cb):
        for table, to in ((UP, 1), (DOWN, 7)):
            dst = table.get(slot)
            if dst is None or (dst == 7 and cb != (0 if table is UP else 1)):
                continue
            ring[dst, cb] = push(
                gk.at[slot, cb], gk.at[dst, cb], dev(y=yd[to]), rsem.at[ring_recv[dst, cb]]
            )

    for cb in range(2):
        arrival(gk.at[0, cb], rsem.at[g0 + cb]).wait()
        forward(0, cb)

    local.wait()
    for one in x_h:
        one.wait()
    x_x = []
    for d in (1, 3, 2):
        x_x.append(
            push(
                xk.at[pl.ds(x * NH, NH)], xk.at[pl.ds(x * NH, NH)], dev(x=xd[d]),
                rsem.at[new_recv()], xk.at[pl.ds(xd[NX - d] * NH, NH)],
            )
        )

    for cb in range(2):
        arrival(qk.at[cb, c * NY + y], rsem.at[q0 + cb]).wait()
    q_y = []
    for d in (1, 7, 2, 6, 3, 5, 4):
        q_y.append(
            push(
                qk.at[:, c * NY + y], qk.at[:, c * NY + y], dev(y=yd[d]),
                rsem.at[new_recv()], qk.at[:, c * NY + yd[NY - d]],
            )
        )

    def x_piece(d, recv):
        at = xd[(NX - d) % NX]
        rows = xk[pl.ds(at * NH, NH)].reshape(NH * 72, 512)
        for jc in range(2):
            part = jnp.dot(rows, bi2[jc], preferred_element_type=F32)
            part = part.astype(BF).reshape(2, 2, 72, 256)
            px[at, :, :, jc] = part
        return push(px.at[at, :, 1 - a], rzx.at[at], dev(a=1 - a), rsem.at[recv])

    x_z_recv = new_recv(NX)
    bi_local.wait()
    bi_other.wait()
    x_z = {}
    x_z[0] = x_piece(0, x_z_recv + x)

    def product(lhs_rows, s0, ns):
        def body(i, _):
            total = None
            for cb in range(2):
                left = bt[cb, pl.ds(pl.multiple_of(i * 224, 8), 224), :]
                part = lax.dot_general(left, lhs_rows[cb], NT, preferred_element_type=F32)
                total = part if total is None else total + part
            for k in range(ns):
                tile = total[:, k * 128 : (k + 1) * 128].reshape(NH, 56, 128)
                pt[s0 + k, pl.ds(i * NH, NH)] = tile.astype(BF)
            return 0

        lax.fori_loop(0, NX, body, 0)

    state = {}

    def send_x(s0, ns):
        state[s0, "x"] = [
            push(
                pt.at[pl.ds(s0, ns), pl.ds(xd[d] * NH, NH)], r1.at[d - 1, pl.ds(s0, ns)],
                dev(x=xd[d]), rsem.at[new_recv()],
            )
            for d in (1, 3, 2)
        ]

    def b1(k):
        s0, ns = CHUNKS[k]
        for s in range(s0, s0 + ns):
            for cb in range(2):
                if s > 0:
                    ring[s, cb].wait()
                    forward(s, cb)
        rows = [gk[s0 : s0 + ns, cb].reshape(ns * 128, 896) for cb in range(2)]
        product(rows, s0, ns)
        send_x(s0, ns)

    def b1q():
        for one in q_y:
            one.wait()
        rows = [qk[cb].astype(F32).reshape(128, 896).astype(BF) for cb in range(2)]
        product(rows, QSLOT, 1)
        send_x(QSLOT, 1)

    def spans(k):
        return (QSLOT, 1) if k == "q" else CHUNKS[k]

    def b2(k):
        s0, ns = spans(k)
        for one in state[s0, "x"]:
            one.wait()
        for s in range(s0, s0 + ns):
            total = pt[s, pl.ds(x * NH, NH)].astype(F32)
            for d in range(3):
                total += r1[d, s].astype(F32)
            s1[s] = total.astype(BF)
        state[s0, "z"] = [
            push(
                s1.at[pl.ds(s0, ns), hd[d]], r2.at[d - 1, pl.ds(s0, ns)],
                dev(h=hd[d]), rsem.at[new_recv()],
            )
            for d in (1, 3, 2)
        ]

    def b3(k):
        s0, ns = spans(k)
        for one in state[s0, "z"]:
            one.wait()
        for s in range(s0, s0 + ns):
            total = s1[s, h].astype(F32)
            for d in range(3):
                total += r2[d, s].astype(F32)
            rg[c, s, x * NH + h] = total.astype(BF)
        mine = rg.at[c, pl.ds(s0, ns), x * NH + h]
        state[s0, "gz"] = [
            push(
                mine, mine, dev(h=hd[d]), rsem.at[new_recv()],
                rg.at[c, pl.ds(s0, ns), x * NH + hd[NH - d]],
            )
            for d in (1, 3, 2)
        ]

    def c2(k):
        s0, ns = spans(k)
        for one in state[s0, "gz"]:
            one.wait()
        mine = rg.at[c, pl.ds(s0, ns), pl.ds(x * NH, NH)]
        state[s0, "gx"] = [
            push(
                mine, mine, dev(x=xd[d]), rsem.at[new_recv()],
                rg.at[c, pl.ds(s0, ns), pl.ds(xd[NX - d] * NH, NH)],
            )
            for d in (1, 3, 2)
        ]

    def c3(k):
        s0, ns = spans(k)
        for one in state[s0, "gx"]:
            one.wait()
        state[s0, "core"] = push(
            rg.at[c, pl.ds(s0, ns)], rg.at[c, pl.ds(s0, ns)], dev(c=1 - c),
            rsem.at[new_recv()], rg.at[1 - c, pl.ds(s0, ns)],
        )

    bt_other.wait()
    b1(0)
    b1q()
    b1(1)
    b2(0)
    b2("q")

    for i, d in enumerate((1, 3, 2)):
        x_x[i].wait()
        x_z[d] = x_piece(d, x_z_recv + xd[NX - d])
    for d in (0, 1, 3, 2):
        at = xd[(NX - d) % NX]
        x_z[d].wait()
        total = px[at, :, a].astype(F32) + rzx[at].astype(F32)
        sx[pl.ds(at * 2, 2)] = total.astype(BF)
    x_y = []
    for d in (1, 7, 2, 6, 3, 5, 4):
        x_y.append(push(sx.at[yd[d]], ryx.at[d - 1], dev(y=yd[d]), rsem.at[new_recv()]))

    b3(0)
    b3("q")
    b1(2)
    b2(1)
    c2(0)
    c2("q")

    for one in x_y:
        one.wait()
    total = sx[y].astype(F32)
    for d in range(7):
        total += ryx[d].astype(F32)
    ox[...] = total.astype(BF)
    rx_recv = new_recv(16)
    rx[c, y, a] = ox[c]
    push(ox.at[1 - c], rx.at[c, y, a], dev(c=1 - c), rsem.at[rx_recv], rx.at[1 - c, y, a])
    rx_in = [arrival(rx.at[1 - c, y, a], rsem.at[rx_recv])]
    for d in (1, 7, 2, 6, 3, 5, 4):
        for same in range(2):
            jc = c if same == 0 else 1 - c
            recv = rsem.at[rx_recv + 1 + (d - 1) * 2 + same]
            push(ox.at[jc], rx.at[c, y, a], dev(y=yd[d], c=jc), recv)
            rx_in.append(arrival(rx.at[jc, yd[NY - d], a], recv))

    b3(1)
    c3(0)
    c3("q")
    b1(3)
    b2(2)
    c2(1)

    for one in rx_in:
        one.wait()
    rx_z = []
    for ch in range(2):
        rx_z.append(
            push(
                rx.at[ch, :, a], rx.at[ch, :, a], dev(a=1 - a),
                rsem.at[new_recv()], rx.at[ch, :, 1 - a],
            )
        )

    b3(2)
    c3(1)
    b1(4)
    b2(3)
    c2(2)
    b3(3)
    b2(4)
    c3(2)
    c2(3)
    b3(4)
    for one in rx_z:
        one.wait()
    for n in range(2):
        for s in range(8):
            shard = n * NY + wrap(y + OFFSETS[s], NY)
            for ch in range(2):
                at = s * 128 + ch * 64
                xf[n, at : at + 64] = rx[ch, lax.div(shard, 2), lax.rem(shard, 2), 0:64]
    c3(3)
    c2(4)
    c3(4)
    for k in (0, 1, 2, 3, 4, "q"):
        state[spans(k)[0], "core"].wait()

    right = rx[0, :, :, 64:72].astype(F32) + rx[1, :, :, 64:72].astype(F32)
    right = right.reshape(128, 256)
    row_query = lax.broadcasted_iota(jnp.int32, (128, 256), 0) // 32
    right = jnp.concatenate(
        [jnp.where(row_query == k, right, 0.0).astype(BF) for k in range(4)], axis=1
    )

    def finish(i, _):
        piece = pl.ds(i * NH, NH)
        squares = None
        for n in range(2):
            left = jnp.concatenate(
                [rg[n, s, piece].reshape(224, 128) for s in range(8)], axis=1
            )
            rotated = jnp.dot(left, xf[n], preferred_element_type=F32)
            squares = rotated * rotated if squares is None else squares + rotated * rotated
        values = squares * (1.0 / 2048.0)
        rows = pl.ds(pl.multiple_of(i * 224, 8), 224)
        eig[rows] = values
        scale = 1.0 / (values + damp[0])
        left = (rg[0, QSLOT, piece] + rg[1, QSLOT, piece]).reshape(224, 128)
        products = jnp.dot(left, right, preferred_element_type=F32)
        for k in range(4):
            pre[k, rows] = (products[:, k * 256 : (k + 1) * 256] * scale).astype(BF)
        return 0

    lax.fori_loop(0, NX, finish, 0)

    @pl.when(c != a)
    def _():
        for copy in to_other_core():
            copy.wait_send()

    for copy in sent:
        copy.wait_send()


def shards(out_grads, inputs, out_basis, in_basis, query_out, query_in, damping):
    c = lax.rem(lax.axis_index("mp"), 2)
    zero = jnp.zeros_like(query_in)
    packed = jnp.concatenate(
        [
            inputs,
            jnp.where(c == 0, query_in, zero),
            jnp.where(c == 1, query_in, zero),
        ],
        axis=0,
    )
    vmem = pl.BlockSpec(memory_space=pltpu.VMEM)
    return pl.pallas_call(
        kernel,
        out_shape=(
            jax.ShapeDtypeStruct((896, 256), F32),
            jax.ShapeDtypeStruct((4, 896, 256), BF),
        ),
        in_specs=[vmem] * 5 + [pl.BlockSpec(memory_space=pltpu.SMEM)],
        out_specs=(vmem, vmem),
        scratch_shapes=[
            pltpu.VMEM((8, 2, 128, 896), BF),
            pltpu.VMEM((2, 16, 8, 896), BF),
            pltpu.VMEM((2, 896, 896), BF),
            pltpu.VMEM((2, 512, 256), BF),
            pltpu.VMEM((9, 16, 56, 128), BF),
            pltpu.VMEM((3, 9, 4, 56, 128), BF),
            pltpu.VMEM((9, 4, 56, 128), BF),
            pltpu.VMEM((3, 9, 56, 128), BF),
            pltpu.VMEM((2, 9, 16, 56, 128), BF),
            pltpu.VMEM((16, 72, 512), BF),
            pltpu.VMEM((4, 2, 2, 2, 72, 256), BF),
            pltpu.VMEM((4, 2, 2, 72, 256), BF),
            pltpu.VMEM((8, 2, 72, 256), BF),
            pltpu.VMEM((7, 2, 72, 256), BF),
            pltpu.VMEM((2, 72, 256), BF),
            pltpu.VMEM((2, 8, 2, 72, 256), BF),
            pltpu.VMEM((2, 1024, 256), BF),
            pltpu.SemaphoreType.DMA((N_SEND,)),
            pltpu.SemaphoreType.DMA((N_RECV,)),
        ],
        compiler_params=pltpu.CompilerParams(
            collective_id=0, has_side_effects=True, vmem_limit_bytes=60 * 1024 * 1024
        ),
    )(out_grads, query_out, out_basis, packed, in_basis, damping)


def solution(mesh):
    placed = (
        P("dp", "mp"),
        P("mp", "dp"),
        P("mp", "dp"),
        P("dp", "mp"),
        P("dp", "mp"),
        P("mp", "dp"),
        P(),
    )
    return jax.shard_map(
        shards,
        mesh=mesh,
        in_specs=placed,
        out_specs=(P("dp", "mp"), P(None, "dp", "mp")),
        check_vma=False,
    )
```

```python
import jax
import jax.numpy as jnp
from jax import lax
from jax.experimental import pallas as pl
from jax.experimental.pallas import tpu as pltpu
from jax.sharding import PartitionSpec as P

BF = jnp.bfloat16
F32 = jnp.float32
MESH = pl.DeviceIdType.MESH
NT = (((1,), (1,)), ((), ()))

NY, NX, NH = 8, 4, 4
CHUNKS = ((0, 1), (1, 2), (3, 2), (5, 2), (7, 1))
QSLOT = 8
OFFSETS = (0, -1, 1, -2, 2, -3, 3, 4)
UP = {0: 1, 1: 3, 3: 5, 5: 7}
DOWN = {0: 2, 2: 4, 4: 6, 6: 7}
N_SEND, N_RECV = 23, 113

ORDER = (
    "x0", "g0", "bt", "rb0", "h1", "q0", "ra12", "b1_0", "h2", "rb12", "q12", "h3", "bi", "bx_0", "b1_1",
    "ra34", "bx_1", "xs1", "rb34", "q34", "by_0", "b1_2", "by_1", "xs2", "xs3", "b2_0", "bx_2", "ra56", "b2_1",
    "rb56", "q56", "xm", "b1_3", "b3_0", "by_2", "b3_1", "bx_3", "r7", "xy", "b1_4", "q7", "b1_q", "c2_0",
    "b2_2", "by_3", "bx_4", "bx_q", "c2_1", "cy_0", "b3_2", "b2_3", "by_4", "by_q", "c3_0", "cy_1", "c2_2",
    "b2_4", "b2_q", "xo", "b3_3", "c3_1", "b3_4", "b3_q", "cy_2", "xz17", "c2_3", "xz26", "c2_4", "c2_q",
    "c3_2", "cy_3", "xz354", "cy_4", "cy_q", "c3_3", "c3_4", "c3_q", "c4_0", "c4_1", "c4_2", "xf", "fin",
    "c4_3", "c4_4", "c4_q",
)


def kernel(
    g, q, b, xi, qi, bi, rg_out, xf_out, right_out,
    gk, qk, bv, bt, bix, pf, ps, pr, pt, rf, pa, r1, s1, r2, rg,
    xc, xk, sx, ryx, rx, xf, right_v,
    ssem, rsem,
):
    dp, mp = lax.axis_index("dp"), lax.axis_index("mp")
    a, y = lax.div(dp, NY), lax.rem(dp, NY)
    x, h, c = lax.div(mp, 8), lax.rem(lax.div(mp, 2), NH), lax.rem(mp, 2)
    m = x * NH + h

    def dev(a=a, y=y, x=x, h=h, c=c):
        return {"dp": a * NY + y, "mp": (x * NH + h) * 2 + c}

    def wrap(v, n):
        return lax.rem(v + n, n)

    yd = [y] + [wrap(y + d, NY) for d in range(1, NY)]
    xd = [x] + [wrap(x + d, NX) for d in range(1, NX)]
    hd = [h] + [wrap(h + d, NH) for d in range(1, NH)]
    counts = [0, 0]
    state = {}
    outs = []

    sends = {}

    def send_sem(kind):
        if kind not in sends:
            assert len(sends) < N_SEND
            sends[kind] = len(sends)
        return ssem.at[sends[kind]]

    def new_recv(n=1):
        counts[1] += n
        assert counts[1] <= N_RECV, counts
        return counts[1] - n

    def arrival(landing, recv):
        return pltpu.make_async_copy(landing, landing, recv)

    def push(kind, src, dst, to, landing, recv=None):
        recv = rsem.at[new_recv()] if recv is None else recv
        pltpu.make_async_remote_copy(
            src_ref=src, dst_ref=dst, send_sem=send_sem(kind), recv_sem=recv,
            device_id=to, device_id_type=MESH,
        ).start()
        return (landing, recv)

    def wait(key):
        for landing, recv in state.pop(key):
            arrival(landing, recv).wait()

    out_recv = new_recv(3)
    load_b = pltpu.make_async_copy(b, bv, rsem.at[new_recv()])
    load_b.start()
    load_bi = pltpu.make_async_copy(bi, bix.at[a], rsem.at[new_recv()])
    load_bi.start()
    factors = qi[...].astype(F32)
    factors = jnp.concatenate([factors, factors], axis=0)
    row_core = lax.broadcasted_iota(jnp.int32, (8, 512), 0) // 4
    xc[0:64] = xi[...]
    xc[64:72] = jnp.where(row_core == c, factors, 0.0).astype(BF)

    barrier = pltpu.get_barrier_semaphore()
    partners = [dev(c=1 - c), dev(a=1 - a), dev(a=1 - a, c=1 - c), dev(y=yd[1]), dev(y=yd[7])]
    partners += [dev(h=hd[1]), dev(h=hd[3]), dev(x=xd[1]), dev(x=xd[3]), dev(x=xd[2])]
    for to in partners:
        pl.semaphore_signal(barrier, inc=1, device_id=to, device_id_type=MESH)
    pl.semaphore_wait(barrier, len(partners))

    x0_recv = rsem.at[new_recv()]
    x0_send = send_sem("x0")

    def x0_other():
        return pltpu.make_async_remote_copy(
            src_ref=xc, dst_ref=xk.at[1 - c, m], send_sem=x0_send, recv_sem=x0_recv,
            device_id=dev(a=1 - a, c=1 - c), device_id_type=MESH,
        )

    def st_x0():
        @pl.when(c == a)
        def _():
            pltpu.make_async_copy(xc, xk.at[c, m], x0_recv).start()

        @pl.when(c != a)
        def _():
            x0_other().start()

        state["x0"] = [(xk.at[c, m], x0_recv)]

    own_recv = new_recv(2)

    def neighbours(slot, half):
        for table, to in ((UP, 1), (DOWN, 7)):
            dst = table.get(slot)
            if dst is None or (dst == 7 and half != (0 if table is UP else 1)):
                continue
            yield dst, dev(y=yd[to])

    def st_g0():
        for dst, to in neighbours(0, 0):
            state["ring", dst, 0] = [push("ring", g, gk.at[dst, a], to, gk.at[dst, a])]
        pltpu.make_async_copy(g, gk.at[0, a], rsem.at[own_recv]).start()
        pltpu.make_async_copy(q, qk.at[a, y], rsem.at[own_recv + 1]).start()
        state["own"] = [(gk.at[0, a], rsem.at[own_recv])]
        state["q", 0] = [(qk.at[a, y], rsem.at[own_recv + 1])]
        state["ring", 0, 1] = [push("gz0", g, gk.at[0, a], dev(a=1 - a), gk.at[0, 1 - a])]
        state["q", 0].append(push("qz0", q, qk.at[a, y], dev(a=1 - a), qk.at[1 - a, y]))

    def st_h1():
        wait("x0")
        mine = xk.at[c, m]
        for d in (1, 3):
            state["h", d] = [
                push("h1", mine, mine, dev(h=hd[d]), xk.at[c, x * NH + hd[NH - d]])
            ]

    def st_h2():
        far = x * NH + hd[2]
        recv = rsem.at[new_recv()]
        for d, rows in ((1, pl.ds(0, 40)), (3, pl.ds(40, 32))):
            wait(("h", d))
            part = xk.at[c, x * NH + hd[NH - d], rows]
            push("h2", part, part, dev(h=hd[d]), None, recv)
        state["h2"] = [(xk.at[c, far], recv)]

    def x_rows(at, rows=None):
        return pl.ds(at * NH, NH) if rows is None else pl.ds(at * NH + 2 * rows, 2)

    def to_core(rows):
        part = xk.at[c, rows]
        return push("xc", part, part, dev(c=1 - c), xk.at[1 - c, rows])

    def st_h3():
        wait("h2")
        mine = xk.at[c, x_rows(x)]
        for d in (1, 3):
            state["x", d] = [
                push("h3", mine, mine, dev(x=xd[d]), xk.at[c, x_rows(xd[NX - d])])
            ]
        state["xc", 0] = [to_core(x_rows(x))]

    def st_xs1():
        recv = rsem.at[new_recv()]
        for i, d in enumerate((1, 3)):
            wait(("x", d))
            part = xk.at[c, x_rows(xd[NX - d], i)]
            push("x2", part, part, dev(x=xd[d]), None, recv)
        state["x2"] = [(xk.at[c, x_rows(xd[2])], recv)]
        for d in (1, 3):
            state["xc", d] = [to_core(x_rows(xd[d]))]

    def x_piece(at):
        total = None
        for fb in range(2):
            rows = xk[fb, x_rows(at)].reshape(NH * 72, 512)
            part = jnp.dot(rows, bix[fb], preferred_element_type=F32)
            total = part if total is None else total + part
        sx[x_rows(at)] = total.astype(BF).reshape(NH, 72, 256)

    def st_bi():
        load_bi.wait()
        state["bi"] = [push("bi", bix.at[a], bix.at[a], dev(a=1 - a), bix.at[1 - a])]

    def st_xs2():
        wait("bi")
        for d in (0, 1, 3):
            wait(("xc", d))
            x_piece(xd[d])

    def st_xs3():
        wait("x2")
        state["xc", 2] = [to_core(x_rows(xd[2]))]

    def st_xm():
        wait(("xc", 2))
        x_piece(xd[2])

    def pair(at):
        return pl.ds(2 * at, 2)

    def st_xy():
        recv = rsem.at[new_recv()]
        for d in (1, 7, 2, 6, 3, 5, 4):
            push("xy", sx.at[pair(yd[d])], ryx.at[d - 1], dev(y=yd[d]), None, recv)
        state["xy"] = [(ryx, recv)]

    def st_xo():
        wait("xy")
        total = sx[pair(y)].astype(F32)
        for d in range(7):
            total += ryx[d].astype(F32)
        rx[a, pair(y)] = total.astype(BF)
        mine = rx.at[a, pair(y)]
        for d in (1, 7, 2, 6, 3, 5, 4):
            landing = rx.at[a, pair(yd[NY - d])]
            state["xo", d] = [push("xo", mine, mine, dev(y=yd[d]), landing)]
        recv = rsem.at[new_recv()]
        state["xz"] = [(rx.at[1 - a], recv)]
        push("xz", mine, mine, dev(a=1 - a), None, recv)

    def st_xz(ds):
        recv = state["xz"][0][1]
        for d in ds:
            wait(("xo", d))
            part = rx.at[a, pair(yd[NY - d])]
            push("xz", part, part, dev(a=1 - a), None, recv)

    def st_xf():
        wait("xz")
        for n in range(2):
            for s in range(8):
                shard = n * NY + wrap(y + OFFSETS[s], NY)
                for half in range(2):
                    at = s * 128 + half * 64
                    xf[n, at : at + 64] = rx[half, shard, 0:64]

    def st_bt():
        eye = (
            lax.broadcasted_iota(jnp.int32, (128, 128), 0)
            == lax.broadcasted_iota(jnp.int32, (128, 128), 1)
        ).astype(F32).astype(BF)
        load_b.wait()
        for j in range(7):
            cols = slice(j * 128, (j + 1) * 128)
            block = lax.dot_general(eye, bv[:, cols], NT, preferred_element_type=F32)
            bt[cols, :] = block.astype(BF)

    def st_ring(half, slots):
        n = a if half == 0 else 1 - a
        for slot in slots:
            wait(("ring", slot, half))
            for dst, to in neighbours(slot, half):
                state["ring", dst, half] = [
                    push("ring", gk.at[slot, n], gk.at[dst, n], to, gk.at[dst, n])
                ]

    def st_q(slots):
        for slot in slots:
            wait(("q", slot))
            mine = qk.at[:, wrap(y + OFFSETS[slot], NY)]
            for dst, to in neighbours(slot, 0):
                landing = qk.at[:, wrap(y + OFFSETS[dst], NY)]
                state["q", dst] = [push("q", mine, mine, to, landing)]

    def product(rows, s0, ns):
        def body(i, _):
            left = bt[pl.ds(pl.multiple_of(i * 224, 8), 224), :]
            terms = lax.dot_general(left, rows, NT, preferred_element_type=F32)
            for k in range(2 * ns):
                tile = terms[:, k * 128 : (k + 1) * 128].reshape(NH, 56, 128)
                if k < ns:
                    pf[s0 + k, pl.ds(i * NH, NH)] = tile
                else:
                    ps[s0 + k - ns, pl.ds(i * NH, NH)] = tile.astype(BF)
            return 0

        lax.fori_loop(0, NX, body, 0)
        landing = pr.at[pl.ds(s0, ns)]
        state[s0, "sum"] = [push("sum", ps.at[pl.ds(s0, ns)], landing, dev(c=1 - c), landing)]

    def st_bx(k):
        s0, ns = spans(k)
        wait((s0, "sum"))
        lane_core = lax.broadcasted_iota(jnp.int32, (16, 56, 128), 2) // 64
        for s in range(s0, s0 + ns):
            total = pf[s] + pr[s].astype(F32)
            if k == "q":
                total = jnp.where(lane_core == c, total, 0.0)
            pt[s] = total.astype(BF)
        slots = pl.ds(s0, ns)
        state[s0, "far"] = []
        for i, d in enumerate((1, 3)):
            landing = rf.at[i, slots]
            state[s0, "far"].append(
                push("far", pt.at[slots, rows_of(xd[2], i)], landing, dev(x=xd[d]), landing)
            )
        recv = rsem.at[new_recv()]
        state[s0, "x"] = [(r1.at[:, slots], recv)]
        for i, d in enumerate((1, 3)):
            landing = r1.at[i, slots, pl.ds(2 - 2 * i, 2)]
            push("x", pt.at[slots, rows_of(xd[d], 1 - i)], landing, dev(x=xd[d]), None, recv)

    def spans(k):
        return (QSLOT, 1) if k == "q" else CHUNKS[int(k)]

    def rows_of(at, half):
        return pl.ds(at * NH + 2 * half, 2)

    def st_by(k):
        s0, ns = spans(k)
        slots = pl.ds(s0, ns)
        for i, d in enumerate((1, 3)):
            arrival(*state[s0, "far"][i]).wait()
            for s in range(s0, s0 + ns):
                total = pt[s, rows_of(xd[d], i)].astype(F32) + rf[i, s].astype(F32)
                pa[i, s] = total.astype(BF)
            landing = r1.at[i, slots, pl.ds(2 * i, 2)]
            push("by", pa.at[i, slots], landing, dev(x=xd[d]), None, state[s0, "x"][0][1])
        del state[s0, "far"]

    def st_b1(k):
        s0, ns = spans(k)
        if k == "q":
            rows = qk[...].astype(F32).reshape(128, 896).astype(BF)
            rows = jnp.concatenate([rows, rows], axis=0)
        else:
            if k == "0":
                wait("own")
            rows = [gk[s0 : s0 + ns, n].reshape(ns * 128, 896) for n in (c, 1 - c)]
            rows = jnp.concatenate(rows, axis=0)
        product(rows, s0, ns)

    def st_b2(k):
        s0, ns = spans(k)
        wait((s0, "x"))
        for s in range(s0, s0 + ns):
            total = pt[s, pl.ds(x * NH, NH)].astype(F32)
            for d in range(2):
                total += r1[d, s].astype(F32)
            s1[s] = total.astype(BF)
        recv = rsem.at[new_recv()]
        slots = pl.ds(s0, ns)
        for d in (1, 3, 2):
            push("z", s1.at[slots, hd[d]], r2.at[d - 1, slots], dev(h=hd[d]), None, recv)
        state[s0, "z"] = [(r2.at[:, slots], recv)]

    def st_b3(k):
        s0, ns = spans(k)
        wait((s0, "z"))
        for s in range(s0, s0 + ns):
            total = s1[s, h].astype(F32)
            for d in range(3):
                total += r2[d, s].astype(F32)
            rg[c, s, m] = total.astype(BF)
        mine = rg.at[c, pl.ds(s0, ns), m]
        recv = rsem.at[new_recv()]
        for d in (1, 3, 2):
            push("gz", mine, mine, dev(h=hd[d]), None, recv)
        state[s0, "gz"] = [(r2.at[:, pl.ds(s0, ns)], recv)]

    def st_c2(k):
        s0, ns = spans(k)
        wait((s0, "gz"))
        mine = rg.at[c, pl.ds(s0, ns), pl.ds(x * NH, NH)]
        state[s0, "gx"] = [
            push("gx", mine, mine, dev(x=xd[d]), rg.at[c, pl.ds(s0, ns), pl.ds(xd[NX - d] * NH, NH)])
            for d in (1, 3)
        ]

    def st_cy(k):
        s0, ns = spans(k)
        slots = pl.ds(s0, ns)
        near = state.pop((s0, "gx"))
        recv = rsem.at[new_recv()]
        for i, d in enumerate((1, 3)):
            arrival(*near[i]).wait()
            part = rg.at[c, slots, rows_of(xd[NX - d], i)]
            push("cy", part, part, dev(x=xd[d]), None, recv)
        state[s0, "gx"] = [(rg.at[c, slots, pl.ds(xd[2] * NH, NH)], recv)]

    def out_copy(core, slots):
        pltpu.make_async_copy(
            rg.at[core, slots], rg_out.at[core, slots], rsem.at[out_recv]
        ).start()

    def st_c3(k):
        s0, ns = spans(k)
        slots = pl.ds(s0, ns)
        wait((s0, "gx"))
        mine = rg.at[c, slots]
        state[s0, "core"] = [push("core", mine, mine, dev(c=1 - c), rg.at[1 - c, slots])]
        out_copy(c, slots)

    def st_c4(k):
        s0, ns = spans(k)
        wait((s0, "core"))
        out_copy(1 - c, pl.ds(s0, ns))

    def st_fin():
        right = rx[0, :, 64:72].astype(F32) + rx[1, :, 64:72].astype(F32)
        right = right.reshape(128, 256)
        row_query = lax.broadcasted_iota(jnp.int32, (128, 256), 0) // 32
        for k in range(4):
            block = jnp.where(row_query == k, right, 0.0).astype(BF)
            right_v[:, k * 256 : (k + 1) * 256] = block
        for src, dst in ((xf, xf_out), (right_v, right_out)):
            outs.append(pltpu.make_async_copy(src, dst, rsem.at[out_recv + 1 + len(outs)]))
            outs[-1].start()

    plain = {
        "x0": st_x0, "g0": st_g0, "h1": st_h1, "h2": st_h2, "h3": st_h3, "xs1": st_xs1,
        "bi": st_bi, "xs2": st_xs2, "xs3": st_xs3, "xm": st_xm, "xy": st_xy, "xo": st_xo,
        "xf": st_xf, "bt": st_bt, "fin": st_fin,
    }
    keyed = {"b1": st_b1, "bx": st_bx, "by": st_by, "b2": st_b2, "b3": st_b3,
             "c2": st_c2, "cy": st_cy, "c3": st_c3, "c4": st_c4}
    for name in ORDER:
        with jax.named_scope(name):
            if name in plain:
                plain[name]()
            elif name.startswith("xz"):
                st_xz([int(v) for v in name[2:]])
            elif name.startswith("r"):
                for half in {"ra": (0,), "rb": (1,)}.get(name[:2], (0, 1)):
                    st_ring(half, [int(v) for v in name if v.isdigit()])
            elif name.startswith("q"):
                st_q([int(v) for v in name[1:]])
            else:
                keyed[name[:2]](name[3:])
    assert not state, state

    with jax.named_scope("outw"):
        pltpu.make_async_copy(rg, rg_out, rsem.at[out_recv]).wait()
        for copy in outs:
            copy.wait()

    @pl.when(c != a)
    def _():
        x0_other().wait_send()

    with jax.named_scope("sentw"):
        totals = {
            "ring": gk.at[1:8], "gz0": gk.at[0, 0], "q": qk.at[:, 0:7], "qz0": qk.at[0, 0],
            "h1": xk.at[0, 0:2], "h2": xk.at[0, 0], "h3": xk.at[0, 0:8], "x2": xk.at[0, 0:4],
            "xc": xk.at[0], "bi": bix.at[0], "xy": ryx, "xo": ryx, "xz": rx.at[0],
            "sum": ps, "far": rf, "x": rf, "by": rf, "z": r2, "gz": r2, "gx": r1, "cy": rf,
            "core": rg.at[0],
        }
        for kind, ref in totals.items():
            arrival(ref, ssem.at[sends[kind]]).wait()
        assert set(sends) == set(totals) | {"x0"}


def last_kernel(rg, xf, right, damp, eig, pre):
    squares = None
    for n in range(2):
        left = jnp.concatenate([rg[n, s].reshape(224, 128) for s in range(8)], axis=1)
        rotated = jnp.dot(left, xf[n], preferred_element_type=F32)
        square = rotated * rotated
        squares = square if squares is None else squares + square
    values = squares * (1.0 / 2048.0)
    eig[...] = values
    scale = 1.0 / (values + damp[0])
    left = (rg[0, QSLOT] + rg[1, QSLOT]).reshape(224, 128)
    products = jnp.dot(left, right[...], preferred_element_type=F32)
    for k in range(4):
        pre[k] = (products[:, k * 256 : (k + 1) * 256] * scale).astype(BF)


def shards(out_grads, inputs, out_basis, in_basis, query_out, query_in, damping):
    vmem = pl.BlockSpec(memory_space=pltpu.VMEM)
    hbm = pl.BlockSpec(memory_space=pl.ANY)
    rg, xf, right = pl.pallas_call(
        kernel,
        out_shape=(
            jax.ShapeDtypeStruct((2, 9, 16, 56, 128), BF),
            jax.ShapeDtypeStruct((2, 1024, 256), BF),
            jax.ShapeDtypeStruct((128, 1024), BF),
        ),
        in_specs=[hbm, hbm, hbm, vmem, vmem, hbm],
        out_specs=(hbm, hbm, hbm),
        scratch_shapes=[
            pltpu.VMEM((8, 2, 128, 896), BF),
            pltpu.VMEM((2, 8, 8, 896), BF),
            pltpu.VMEM((896, 896), BF),
            pltpu.VMEM((896, 896), BF),
            pltpu.VMEM((2, 512, 256), BF),
            pltpu.VMEM((9, 16, 56, 128), F32),
            pltpu.VMEM((9, 16, 56, 128), BF),
            pltpu.VMEM((9, 16, 56, 128), BF),
            pltpu.VMEM((9, 16, 56, 128), BF),
            pltpu.VMEM((2, 9, 2, 56, 128), BF),
            pltpu.VMEM((2, 9, 2, 56, 128), BF),
            pltpu.VMEM((2, 9, 4, 56, 128), BF),
            pltpu.VMEM((9, 4, 56, 128), BF),
            pltpu.VMEM((3, 9, 56, 128), BF),
            pltpu.VMEM((2, 9, 16, 56, 128), BF),
            pltpu.VMEM((72, 512), BF),
            pltpu.VMEM((2, 16, 72, 512), BF),
            pltpu.VMEM((16, 72, 256), BF),
            pltpu.VMEM((7, 2, 72, 256), BF),
            pltpu.VMEM((2, 16, 72, 256), BF),
            pltpu.VMEM((2, 1024, 256), BF),
            pltpu.VMEM((128, 1024), BF),
            pltpu.SemaphoreType.DMA((N_SEND,)),
            pltpu.SemaphoreType.DMA((N_RECV,)),
        ],
        compiler_params=pltpu.CompilerParams(
            collective_id=0, has_side_effects=True, vmem_limit_bytes=60 * 1024 * 1024
        ),
    )(out_grads, query_out, out_basis, inputs, query_in, in_basis)
    return pl.pallas_call(
        last_kernel,
        grid=(NX,),
        out_shape=(
            jax.ShapeDtypeStruct((896, 256), F32),
            jax.ShapeDtypeStruct((4, 896, 256), BF),
        ),
        in_specs=[
            pl.BlockSpec((2, 9, NH, 56, 128), lambda i: (0, 0, i, 0, 0)),
            pl.BlockSpec((2, 1024, 256), lambda i: (0, 0, 0)),
            pl.BlockSpec((128, 1024), lambda i: (0, 0)),
            pl.BlockSpec(memory_space=pltpu.SMEM),
        ],
        out_specs=(
            pl.BlockSpec((224, 256), lambda i: (i, 0)),
            pl.BlockSpec((4, 224, 256), lambda i: (0, i, 0)),
        ),
        compiler_params=pltpu.CompilerParams(vmem_limit_bytes=60 * 1024 * 1024),
    )(rg, xf, right, damping)


def solution(mesh):
    placed = (
        P("dp", "mp"),
        P("mp", "dp"),
        P("mp", "dp"),
        P("dp", "mp"),
        P("dp", "mp"),
        P("mp", "dp"),
        P(),
    )
    return jax.shard_map(
        shards,
        mesh=mesh,
        in_specs=placed,
        out_specs=(P("dp", "mp"), P(None, "dp", "mp")),
        check_vma=False,
    )
```

```python
import jax
import jax.numpy as jnp
from jax import lax
from jax.experimental import pallas as pl
from jax.experimental.pallas import tpu as pltpu
from jax.sharding import PartitionSpec as P

BF = jnp.bfloat16
F32 = jnp.float32
MESH = pl.DeviceIdType.MESH
NT = (((1,), (1,)), ((), ()))

NY, NX, NH = 8, 4, 4
CHUNKS = ((0, 1), (1, 2), (3, 2), (5, 2), (7, 1))
QSLOT = 8
OFFSETS = (0, -1, 1, -2, 2, -3, 3, 4)
UP = {0: 1, 1: 3, 3: 5, 5: 7}
DOWN = {0: 2, 2: 4, 4: 6, 6: 7}
N_SEND, N_RECV = 23, 113

ORDER = (
    "x0", "g0", "bt", "rb0", "h1", "q0", "ra12", "b1_0", "h2", "rb12", "q12", "h3", "bi", "bx_0", "b1_1",
    "ra34", "bx_1", "xs1", "rb34", "q34", "by_0", "b1_2", "by_1", "xs2", "xs3", "b2_0", "bx_2", "ra56", "b2_1",
    "rb56", "q56", "xm", "b1_3", "b3_0", "by_2", "b3_1", "bx_3", "r7", "xy", "b1_4", "q7", "b1_q", "c2_0",
    "b2_2", "by_3", "bx_4", "bx_q", "c2_1", "b3_2", "b2_3", "by_4", "by_q", "cy_0", "cy_1", "c2_2", "b2_4",
    "b2_q", "xo", "b3_3", "c3_0", "b3_4", "b3_q", "cy_2", "xz17", "c2_3", "c2_4", "c2_q", "xz26", "c3_1",
    "c3_2", "cy_3", "cy_4", "cy_q", "xz354", "c3_3", "c3_4", "c3_q", "c4_0", "c4_1", "c4_2", "xf", "fin",
    "c4_3", "c4_4", "c4_q",
)


def kernel(
    g, q, b, xi, qi, bi, rg_out, xf_out, right_out,
    gk, qk, bv, bt, bix, pf, ps, pr, pt, rf, pa, r1, s1, r2, rg,
    xc, xk, sx, ryx, rx, xf, right_v,
    ssem, rsem,
):
    dp, mp = lax.axis_index("dp"), lax.axis_index("mp")
    a, y = lax.div(dp, NY), lax.rem(dp, NY)
    x, h, c = lax.div(mp, 8), lax.rem(lax.div(mp, 2), NH), lax.rem(mp, 2)
    m = x * NH + h

    def dev(a=a, y=y, x=x, h=h, c=c):
        return {"dp": a * NY + y, "mp": (x * NH + h) * 2 + c}

    def wrap(v, n):
        return lax.rem(v + n, n)

    yd = [y] + [wrap(y + d, NY) for d in range(1, NY)]
    xd = [x] + [wrap(x + d, NX) for d in range(1, NX)]
    hd = [h] + [wrap(h + d, NH) for d in range(1, NH)]
    counts = [0, 0]
    state = {}
    outs = []

    sends = {}

    def send_sem(kind):
        if kind not in sends:
            assert len(sends) < N_SEND
            sends[kind] = len(sends)
        return ssem.at[sends[kind]]

    def new_recv(n=1):
        counts[1] += n
        assert counts[1] <= N_RECV, counts
        return counts[1] - n

    def arrival(landing, recv):
        return pltpu.make_async_copy(landing, landing, recv)

    def push(kind, src, dst, to, landing, recv=None):
        recv = rsem.at[new_recv()] if recv is None else recv
        pltpu.make_async_remote_copy(
            src_ref=src, dst_ref=dst, send_sem=send_sem(kind), recv_sem=recv,
            device_id=to, device_id_type=MESH,
        ).start()
        return (landing, recv)

    def wait(key):
        for landing, recv in state.pop(key):
            arrival(landing, recv).wait()

    out_recv = new_recv(3)
    load_b = pltpu.make_async_copy(b, bv, rsem.at[new_recv()])
    load_b.start()
    load_bi = pltpu.make_async_copy(bi, bix.at[a], rsem.at[new_recv()])
    load_bi.start()
    factors = qi[...].astype(F32)
    factors = jnp.concatenate([factors, factors], axis=0)
    row_core = lax.broadcasted_iota(jnp.int32, (8, 512), 0) // 4
    xc[0:64] = xi[...]
    xc[64:72] = jnp.where(row_core == c, factors, 0.0).astype(BF)

    barrier = pltpu.get_barrier_semaphore()
    partners = [dev(c=1 - c), dev(a=1 - a), dev(a=1 - a, c=1 - c), dev(y=yd[1]), dev(y=yd[7])]
    partners += [dev(h=hd[1]), dev(h=hd[3]), dev(x=xd[1]), dev(x=xd[3]), dev(x=xd[2])]
    for to in partners:
        pl.semaphore_signal(barrier, inc=1, device_id=to, device_id_type=MESH)
    pl.semaphore_wait(barrier, len(partners))

    x0_recv = rsem.at[new_recv()]
    x0_send = send_sem("x0")

    def x0_other():
        return pltpu.make_async_remote_copy(
            src_ref=xc, dst_ref=xk.at[1 - c, m], send_sem=x0_send, recv_sem=x0_recv,
            device_id=dev(a=1 - a, c=1 - c), device_id_type=MESH,
        )

    def st_x0():
        @pl.when(c == a)
        def _():
            pltpu.make_async_copy(xc, xk.at[c, m], x0_recv).start()

        @pl.when(c != a)
        def _():
            x0_other().start()

        state["x0"] = [(xk.at[c, m], x0_recv)]

    own_recv = new_recv(2)

    def neighbours(slot, half):
        for table, to in ((UP, 1), (DOWN, 7)):
            dst = table.get(slot)
            if dst is None or (dst == 7 and half != (0 if table is UP else 1)):
                continue
            yield dst, dev(y=yd[to])

    def st_g0():
        for dst, to in neighbours(0, 0):
            state["ring", dst, 0] = [push("ring", g, gk.at[dst, a], to, gk.at[dst, a])]
        pltpu.make_async_copy(g, gk.at[0, a], rsem.at[own_recv]).start()
        pltpu.make_async_copy(q, qk.at[a, y], rsem.at[own_recv + 1]).start()
        state["own"] = [(gk.at[0, a], rsem.at[own_recv])]
        state["q", 0] = [(qk.at[a, y], rsem.at[own_recv + 1])]
        state["ring", 0, 1] = [push("gz0", g, gk.at[0, a], dev(a=1 - a), gk.at[0, 1 - a])]
        state["q", 0].append(push("qz0", q, qk.at[a, y], dev(a=1 - a), qk.at[1 - a, y]))

    def st_h1():
        wait("x0")
        mine = xk.at[c, m]
        for d in (1, 3):
            state["h", d] = [
                push("h1", mine, mine, dev(h=hd[d]), xk.at[c, x * NH + hd[NH - d]])
            ]

    def st_h2():
        far = x * NH + hd[2]
        recv = rsem.at[new_recv()]
        for d, rows in ((1, pl.ds(0, 40)), (3, pl.ds(40, 32))):
            wait(("h", d))
            part = xk.at[c, x * NH + hd[NH - d], rows]
            push("h2", part, part, dev(h=hd[d]), None, recv)
        state["h2"] = [(xk.at[c, far], recv)]

    def x_rows(at, rows=None):
        return pl.ds(at * NH, NH) if rows is None else pl.ds(at * NH + 2 * rows, 2)

    def to_core(rows):
        part = xk.at[c, rows]
        return push("xc", part, part, dev(c=1 - c), xk.at[1 - c, rows])

    def st_h3():
        wait("h2")
        mine = xk.at[c, x_rows(x)]
        for d in (1, 3):
            state["x", d] = [
                push("h3", mine, mine, dev(x=xd[d]), xk.at[c, x_rows(xd[NX - d])])
            ]
        state["xc", 0] = [to_core(x_rows(x))]

    def st_xs1():
        recv = rsem.at[new_recv()]
        for i, d in enumerate((1, 3)):
            wait(("x", d))
            part = xk.at[c, x_rows(xd[NX - d], i)]
            push("x2", part, part, dev(x=xd[d]), None, recv)
        state["x2"] = [(xk.at[c, x_rows(xd[2])], recv)]
        for d in (1, 3):
            state["xc", d] = [to_core(x_rows(xd[d]))]

    def x_piece(at):
        total = None
        for fb in range(2):
            rows = xk[fb, x_rows(at)].reshape(NH * 72, 512)
            part = jnp.dot(rows, bix[fb], preferred_element_type=F32)
            total = part if total is None else total + part
        sx[x_rows(at)] = total.astype(BF).reshape(NH, 72, 256)

    def st_bi():
        load_bi.wait()
        state["bi"] = [push("bi", bix.at[a], bix.at[a], dev(a=1 - a), bix.at[1 - a])]

    def st_xs2():
        wait("bi")
        for d in (0, 1, 3):
            wait(("xc", d))
            x_piece(xd[d])

    def st_xs3():
        wait("x2")
        state["xc", 2] = [to_core(x_rows(xd[2]))]

    def st_xm():
        wait(("xc", 2))
        x_piece(xd[2])

    def pair(at):
        return pl.ds(2 * at, 2)

    def st_xy():
        recv = rsem.at[new_recv()]
        for d in (1, 7, 2, 6, 3, 5, 4):
            push("xy", sx.at[pair(yd[d])], ryx.at[d - 1], dev(y=yd[d]), None, recv)
        state["xy"] = [(ryx, recv)]

    def st_xo():
        wait("xy")
        total = sx[pair(y)].astype(F32)
        for d in range(7):
            total += ryx[d].astype(F32)
        rx[a, pair(y)] = total.astype(BF)
        mine = rx.at[a, pair(y)]
        for d in (1, 7, 2, 6, 3, 5, 4):
            landing = rx.at[a, pair(yd[NY - d])]
            state["xo", d] = [push("xo", mine, mine, dev(y=yd[d]), landing)]
        recv = rsem.at[new_recv()]
        state["xz"] = [(rx.at[1 - a], recv)]
        push("xz", mine, mine, dev(a=1 - a), None, recv)

    def st_xz(ds):
        recv = state["xz"][0][1]
        for d in ds:
            wait(("xo", d))
            part = rx.at[a, pair(yd[NY - d])]
            push("xz", part, part, dev(a=1 - a), None, recv)

    def st_xf():
        wait("xz")
        for n in range(2):
            for s in range(8):
                shard = n * NY + wrap(y + OFFSETS[s], NY)
                for half in range(2):
                    at = s * 128 + half * 64
                    xf[n, at : at + 64] = rx[half, shard, 0:64]

    def st_bt():
        eye = (
            lax.broadcasted_iota(jnp.int32, (128, 128), 0)
            == lax.broadcasted_iota(jnp.int32, (128, 128), 1)
        ).astype(F32).astype(BF)
        load_b.wait()
        for j in range(7):
            cols = slice(j * 128, (j + 1) * 128)
            block = lax.dot_general(eye, bv[:, cols], NT, preferred_element_type=F32)
            bt[cols, :] = block.astype(BF)

    def st_ring(half, slots):
        n = a if half == 0 else 1 - a
        for slot in slots:
            wait(("ring", slot, half))
            for dst, to in neighbours(slot, half):
                state["ring", dst, half] = [
                    push("ring", gk.at[slot, n], gk.at[dst, n], to, gk.at[dst, n])
                ]

    def st_q(slots):
        for slot in slots:
            wait(("q", slot))
            mine = qk.at[:, wrap(y + OFFSETS[slot], NY)]
            for dst, to in neighbours(slot, 0):
                landing = qk.at[:, wrap(y + OFFSETS[dst], NY)]
                state["q", dst] = [push("q", mine, mine, to, landing)]

    def product(rows, s0, ns):
        def body(i, _):
            left = bt[pl.ds(pl.multiple_of(i * 224, 8), 224), :]
            terms = lax.dot_general(left, rows, NT, preferred_element_type=F32)
            for k in range(2 * ns):
                tile = terms[:, k * 128 : (k + 1) * 128].reshape(NH, 56, 128)
                if k < ns:
                    pf[s0 + k, pl.ds(i * NH, NH)] = tile
                else:
                    ps[s0 + k - ns, pl.ds(i * NH, NH)] = tile.astype(BF)
            return 0

        lax.fori_loop(0, NX, body, 0)
        landing = pr.at[pl.ds(s0, ns)]
        state[s0, "sum"] = [push("sum", ps.at[pl.ds(s0, ns)], landing, dev(c=1 - c), landing)]

    def st_bx(k):
        s0, ns = spans(k)
        wait((s0, "sum"))
        lane_core = lax.broadcasted_iota(jnp.int32, (16, 56, 128), 2) // 64
        for s in range(s0, s0 + ns):
            total = pf[s] + pr[s].astype(F32)
            if k == "q":
                total = jnp.where(lane_core == c, total, 0.0)
            pt[s] = total.astype(BF)
        slots = pl.ds(s0, ns)
        state[s0, "far"] = []
        for i, d in enumerate((1, 3)):
            landing = rf.at[i, slots]
            state[s0, "far"].append(
                push("far", pt.at[slots, rows_of(xd[2], i)], landing, dev(x=xd[d]), landing)
            )
        recv = rsem.at[new_recv()]
        state[s0, "x"] = [(r1.at[:, slots], recv)]
        for i, d in enumerate((1, 3)):
            landing = r1.at[i, slots, pl.ds(2 - 2 * i, 2)]
            push("x", pt.at[slots, rows_of(xd[d], 1 - i)], landing, dev(x=xd[d]), None, recv)

    def spans(k):
        return (QSLOT, 1) if k == "q" else CHUNKS[int(k)]

    def rows_of(at, half):
        return pl.ds(at * NH + 2 * half, 2)

    def st_by(k):
        s0, ns = spans(k)
        slots = pl.ds(s0, ns)
        for i, d in enumerate((1, 3)):
            arrival(*state[s0, "far"][i]).wait()
            for s in range(s0, s0 + ns):
                total = pt[s, rows_of(xd[d], i)].astype(F32) + rf[i, s].astype(F32)
                pa[i, s] = total.astype(BF)
            landing = r1.at[i, slots, pl.ds(2 * i, 2)]
            push("by", pa.at[i, slots], landing, dev(x=xd[d]), None, state[s0, "x"][0][1])
        del state[s0, "far"]

    def st_b1(k):
        s0, ns = spans(k)
        if k == "q":
            rows = qk[...].astype(F32).reshape(128, 896).astype(BF)
            rows = jnp.concatenate([rows, rows], axis=0)
        else:
            if k == "0":
                wait("own")
            rows = [gk[s0 : s0 + ns, n].reshape(ns * 128, 896) for n in (c, 1 - c)]
            rows = jnp.concatenate(rows, axis=0)
        product(rows, s0, ns)

    def st_b2(k):
        s0, ns = spans(k)
        wait((s0, "x"))
        for s in range(s0, s0 + ns):
            total = pt[s, pl.ds(x * NH, NH)].astype(F32)
            for d in range(2):
                total += r1[d, s].astype(F32)
            s1[s] = total.astype(BF)
        recv = rsem.at[new_recv()]
        slots = pl.ds(s0, ns)
        for d in (1, 3, 2):
            push("z", s1.at[slots, hd[d]], r2.at[d - 1, slots], dev(h=hd[d]), None, recv)
        state[s0, "z"] = [(r2.at[:, slots], recv)]

    def st_b3(k):
        s0, ns = spans(k)
        wait((s0, "z"))
        for s in range(s0, s0 + ns):
            total = s1[s, h].astype(F32)
            for d in range(3):
                total += r2[d, s].astype(F32)
            rg[s, m] = total.astype(BF)
        mine = rg.at[pl.ds(s0, ns), m]
        recv = rsem.at[new_recv()]
        for d in (1, 3, 2):
            push("gz", mine, mine, dev(h=hd[d]), None, recv)
        state[s0, "gz"] = [(r2.at[:, pl.ds(s0, ns)], recv)]

    def st_c2(k):
        s0, ns = spans(k)
        wait((s0, "gz"))
        mine = rg.at[pl.ds(s0, ns), pl.ds(x * NH, NH)]
        state[s0, "gx"] = [
            push("gx", mine, mine, dev(x=xd[d]), rg.at[pl.ds(s0, ns), pl.ds(xd[NX - d] * NH, NH)])
            for d in (1, 3)
        ]

    def st_cy(k):
        s0, ns = spans(k)
        slots = pl.ds(s0, ns)
        near = state.pop((s0, "gx"))
        recv = rsem.at[new_recv()]
        for i, d in enumerate((1, 3)):
            arrival(*near[i]).wait()
            part = rg.at[slots, rows_of(xd[NX - d], i)]
            push("cy", part, part, dev(x=xd[d]), None, recv)
        state[s0, "gx"] = [(rg.at[slots, pl.ds(xd[2] * NH, NH)], recv)]

    def st_c3(k):
        s0, ns = spans(k)
        slots = pl.ds(s0, ns)
        wait((s0, "gx"))
        mine = rg.at[slots]
        state[s0, "core"] = [
            push("core", mine, rg_out.at[c, slots], dev(c=1 - c), rg_out.at[1 - c, slots])
        ]
        pltpu.make_async_copy(mine, rg_out.at[c, slots], rsem.at[out_recv]).start()

    def st_c4(k):
        s0, ns = spans(k)
        wait((s0, "core"))

    def st_fin():
        right = rx[0, :, 64:72].astype(F32) + rx[1, :, 64:72].astype(F32)
        right = right.reshape(128, 256)
        row_query = lax.broadcasted_iota(jnp.int32, (128, 256), 0) // 32
        for k in range(4):
            block = jnp.where(row_query == k, right, 0.0).astype(BF)
            right_v[:, k * 256 : (k + 1) * 256] = block
        for src, dst in ((xf, xf_out), (right_v, right_out)):
            outs.append(pltpu.make_async_copy(src, dst, rsem.at[out_recv + 1 + len(outs)]))
            outs[-1].start()

    plain = {
        "x0": st_x0, "g0": st_g0, "h1": st_h1, "h2": st_h2, "h3": st_h3, "xs1": st_xs1,
        "bi": st_bi, "xs2": st_xs2, "xs3": st_xs3, "xm": st_xm, "xy": st_xy, "xo": st_xo,
        "xf": st_xf, "bt": st_bt, "fin": st_fin,
    }
    keyed = {"b1": st_b1, "bx": st_bx, "by": st_by, "b2": st_b2, "b3": st_b3,
             "c2": st_c2, "cy": st_cy, "c3": st_c3, "c4": st_c4}
    for name in ORDER:
        with jax.named_scope(name):
            if name in plain:
                plain[name]()
            elif name.startswith("xz"):
                st_xz([int(v) for v in name[2:]])
            elif name.startswith("r"):
                for half in {"ra": (0,), "rb": (1,)}.get(name[:2], (0, 1)):
                    st_ring(half, [int(v) for v in name if v.isdigit()])
            elif name.startswith("q"):
                st_q([int(v) for v in name[1:]])
            else:
                keyed[name[:2]](name[3:])
    assert not state, state

    with jax.named_scope("outw"):
        pltpu.make_async_copy(rg, rg_out.at[c], rsem.at[out_recv]).wait()
        for copy in outs:
            copy.wait()

    @pl.when(c != a)
    def _():
        x0_other().wait_send()

    with jax.named_scope("sentw"):
        totals = {
            "ring": gk.at[1:8], "gz0": gk.at[0, 0], "q": qk.at[:, 0:7], "qz0": qk.at[0, 0],
            "h1": xk.at[0, 0:2], "h2": xk.at[0, 0], "h3": xk.at[0, 0:8], "x2": xk.at[0, 0:4],
            "xc": xk.at[0], "bi": bix.at[0], "xy": ryx, "xo": ryx, "xz": rx.at[0],
            "sum": ps, "far": rf, "x": rf, "by": rf, "z": r2, "gz": r2, "gx": r1, "cy": rf,
            "core": rg,
        }
        for kind, ref in totals.items():
            arrival(ref, ssem.at[sends[kind]]).wait()
        assert set(sends) == set(totals) | {"x0"}


def last_kernel(rg, xf, right, damp, eig, pre):
    squares = None
    for n in range(2):
        left = jnp.concatenate([rg[n, s].reshape(448, 128) for s in range(8)], axis=1)
        rotated = jnp.dot(left, xf[n], preferred_element_type=F32)
        square = rotated * rotated
        squares = square if squares is None else squares + square
    values = squares * (1.0 / 2048.0)
    eig[...] = values
    scale = 1.0 / (values + damp[0])
    left = (rg[0, QSLOT] + rg[1, QSLOT]).reshape(448, 128)
    products = jnp.dot(left, right[...], preferred_element_type=F32)
    for k in range(4):
        pre[k] = (products[:, k * 256 : (k + 1) * 256] * scale).astype(BF)


def shards(out_grads, inputs, out_basis, in_basis, query_out, query_in, damping):
    vmem = pl.BlockSpec(memory_space=pltpu.VMEM)
    hbm = pl.BlockSpec(memory_space=pl.ANY)
    rg, xf, right = pl.pallas_call(
        kernel,
        out_shape=(
            jax.ShapeDtypeStruct((2, 9, 16, 56, 128), BF),
            jax.ShapeDtypeStruct((2, 1024, 256), BF),
            jax.ShapeDtypeStruct((128, 1024), BF),
        ),
        in_specs=[hbm, hbm, hbm, vmem, vmem, hbm],
        out_specs=(hbm, hbm, hbm),
        scratch_shapes=[
            pltpu.VMEM((8, 2, 128, 896), BF),
            pltpu.VMEM((2, 8, 8, 896), BF),
            pltpu.VMEM((896, 896), BF),
            pltpu.VMEM((896, 896), BF),
            pltpu.VMEM((2, 512, 256), BF),
            pltpu.VMEM((9, 16, 56, 128), F32),
            pltpu.VMEM((9, 16, 56, 128), BF),
            pltpu.VMEM((9, 16, 56, 128), BF),
            pltpu.VMEM((9, 16, 56, 128), BF),
            pltpu.VMEM((2, 9, 2, 56, 128), BF),
            pltpu.VMEM((2, 9, 2, 56, 128), BF),
            pltpu.VMEM((2, 9, 4, 56, 128), BF),
            pltpu.VMEM((9, 4, 56, 128), BF),
            pltpu.VMEM((3, 9, 56, 128), BF),
            pltpu.VMEM((9, 16, 56, 128), BF),
            pltpu.VMEM((72, 512), BF),
            pltpu.VMEM((2, 16, 72, 512), BF),
            pltpu.VMEM((16, 72, 256), BF),
            pltpu.VMEM((7, 2, 72, 256), BF),
            pltpu.VMEM((2, 16, 72, 256), BF),
            pltpu.VMEM((2, 1024, 256), BF),
            pltpu.VMEM((128, 1024), BF),
            pltpu.SemaphoreType.DMA((N_SEND,)),
            pltpu.SemaphoreType.DMA((N_RECV,)),
        ],
        compiler_params=pltpu.CompilerParams(
            collective_id=0, has_side_effects=True, vmem_limit_bytes=60 * 1024 * 1024
        ),
    )(out_grads, query_out, out_basis, inputs, query_in, in_basis)
    return pl.pallas_call(
        last_kernel,
        grid=(2,),
        out_shape=(
            jax.ShapeDtypeStruct((896, 256), F32),
            jax.ShapeDtypeStruct((4, 896, 256), BF),
        ),
        in_specs=[
            pl.BlockSpec((2, 9, 8, 56, 128), lambda i: (0, 0, i, 0, 0)),
            pl.BlockSpec((2, 1024, 256), lambda i: (0, 0, 0)),
            pl.BlockSpec((128, 1024), lambda i: (0, 0)),
            pl.BlockSpec(memory_space=pltpu.SMEM),
        ],
        out_specs=(
            pl.BlockSpec((448, 256), lambda i: (i, 0)),
            pl.BlockSpec((4, 448, 256), lambda i: (0, i, 0)),
        ),
        compiler_params=pltpu.CompilerParams(vmem_limit_bytes=60 * 1024 * 1024),
    )(rg, xf, right, damping)


def solution(mesh):
    placed = (
        P("dp", "mp"),
        P("mp", "dp"),
        P("mp", "dp"),
        P("dp", "mp"),
        P("dp", "mp"),
        P("mp", "dp"),
        P(),
    )
    return jax.shard_map(
        shards,
        mesh=mesh,
        in_specs=placed,
        out_specs=(P("dp", "mp"), P(None, "dp", "mp")),
        check_vma=False,
    )
```
